256 devices in a mesh: head: 8 (over z), seq: 32 (over y, x, core).
Axes of the slice: x: 4, y: 4, z: 8, core: 2. Of those that a mesh axis runs over, the one named last changes fastest.
Arguments:
- queries: bfloat16 [4096, 8192], P('seq', 'head'), may hold values from -100 to 100
- keys: bfloat16 [4096, 1024], P('seq', 'head'), may hold values from -5 to 5
- values: bfloat16 [4096, 1024], P('seq', 'head'), may hold values from -6 to 6
- q_tangent: bfloat16 [4096, 8192], P('seq', 'head'), may hold values from -6 to 6
- k_tangent: bfloat16 [4096, 1024], P('seq', 'head'), may hold values from -6 to 6
- v_tangent: bfloat16 [4096, 1024], P('seq', 'head'), may hold values from -6 to 6
- out_grad: bfloat16 [4096, 8192], P('seq', 'head'), may hold values from -6 to 6
- block_order: int32 [32], replicated, may hold values from 0 to 31, each once
Outputs:
- dq_tangent: bfloat16 [4096, 8192], P('seq', 'head')
- dk_tangent: bfloat16 [4096, 1024], P('seq', 'head')
- dv_tangent: bfloat16 [4096, 1024], P('seq', 'head')
- squared_norm: float32 [], replicated
The draws below stay inside these ranges and needn't reach their ends.
Inputs may be any that keep to these rules, and one draw needn't show every extreme that they name: `block_order`: every value of 0 to 31 appears once.
All inputs are finite; a program needn't handle non-finite values.
Results may differ from the reference program's by a relative error of at most 0.025.
Values may be sent and summed in bfloat16 or wider, within the bound.
A program may use at most 64 MiB of HBM per device.

```python
import jax
import jax.numpy as jnp
from jax import lax

KVH = 8
HD = 128
G = 8
TOK_DEV = 128
QH = 64
SEQ_LEN = 4096
N_SEQ = 32


def base_keys(key):
    return jnp.clip(jax.random.normal(jax.random.fold_in(key, 3), (SEQ_LEN, KVH * HD), jnp.float32), -5.0, 5.0)


def draw_keys(key, part):
    drawn = base_keys(key)
    return drawn.astype(jnp.bfloat16)


def draw_queries(key, part):
    drawn = jnp.clip(jax.random.normal(jax.random.fold_in(key, 4), (SEQ_LEN, QH * HD), jnp.float32), -5.0, 5.0)
    return drawn.astype(jnp.bfloat16)


def block_levels(own_key, shape, cuts, low, top_value):
    factor_of = 1.0
    for axis_at, blocks in cuts:
        steps = jax.random.uniform(jax.random.fold_in(jax.random.fold_in(own_key, 6), axis_at), (blocks,), jnp.float32, low / len(cuts), top_value / len(cuts))
        factor_of = factor_of * jnp.repeat(jnp.exp(steps), shape[axis_at] // blocks).reshape((-1,) + (1,) * (len(shape) - 1 - axis_at))
    return factor_of


def scatter_about(key, extent, width, most, pieces=(), kind=jnp.bfloat16):
    result = jax.random.normal(key, extent, jnp.float32) * width
    if len(pieces) > 0:
        result = block_levels(key, extent, pieces, -0.22, 0.18) * result
    return jnp.clip(result, min=-most, max=most).astype(kind)


def setup_inputs(seed: int = 0) -> dict:
    arg_keys = jax.random.split(jax.random.key(seed), 9)
    return {
        "queries": draw_queries(jax.random.fold_in(arg_keys[8], 71), 0),
        "keys": draw_keys(jax.random.fold_in(arg_keys[8], 71), 0),
        "values": scatter_about(arg_keys[2], (SEQ_LEN, KVH * HD), 1.0, 6.0, ((0, 32), (1, 8))),
        "q_tangent": scatter_about(arg_keys[3], (SEQ_LEN, QH * HD), 1.0, 6.0, ((0, 32), (1, 8))),
        "k_tangent": scatter_about(arg_keys[4], (SEQ_LEN, KVH * HD), 1.0, 6.0, ((0, 32), (1, 8))),
        "v_tangent": scatter_about(arg_keys[5], (SEQ_LEN, KVH * HD), 1.0, 6.0, ((0, 32), (1, 8))),
        "out_grad": scatter_about(arg_keys[6], (SEQ_LEN, QH * HD), 1.0, 6.0, ((0, 32), (1, 8))),
        "block_order": jax.random.permutation(arg_keys[7], N_SEQ).astype(jnp.int32),
    }


neg_fill = -1e30


def rounded(value):
    return lax.optimization_barrier(value.astype(jnp.bfloat16)).astype(jnp.float32)


def reference(queries, keys, values, q_tangent, k_tangent, v_tangent, out_grad, block_order):
    scaling = HD ** -0.5
    positions = (block_order[:, None] * TOK_DEV + jnp.arange(TOK_DEV, dtype=jnp.int32)[None, :]).reshape(-1).astype(jnp.int32)
    key_full = keys.astype(jnp.float32).reshape(SEQ_LEN, KVH, HD)
    val_full = values.astype(jnp.float32).reshape(SEQ_LEN, KVH, HD)
    key_tan = k_tangent.astype(jnp.float32).reshape(SEQ_LEN, KVH, HD)
    val_tan = v_tangent.astype(jnp.float32).reshape(SEQ_LEN, KVH, HD)
    query_block = min(128, SEQ_LEN)
    block_total = SEQ_LEN // query_block

    def split_rows(array):
        return array.astype(jnp.float32).reshape(block_total, query_block, KVH, G, HD)

    inputs = (split_rows(queries), split_rows(q_tangent), split_rows(out_grad), positions.reshape(block_total, query_block))

    def one_block(carry, items):
        dk_acc, dv_acc = carry
        query_rows, query_tan, grad_rows, query_pos = items
        visible = (positions[None, :] <= query_pos[:, None])[None, None]
        s_main = jnp.einsum("thgd,shd->hgts", query_rows, key_full) * scaling
        s_tan = (jnp.einsum("thgd,shd->hgts", query_tan, key_full) + jnp.einsum("thgd,shd->hgts", query_rows, key_tan)) * scaling
        d_prob = jnp.einsum("thgd,shd->hgts", grad_rows, val_full)
        d_prob_tan = jnp.einsum("thgd,shd->hgts", grad_rows, val_tan)
        row_max = jnp.max(jnp.where(visible, s_main, neg_fill), axis=-1, keepdims=True)
        expo = jnp.where(visible, jnp.exp(s_main - row_max), 0.0)
        prob = expo / jnp.sum(expo, axis=-1, keepdims=True)
        tan_mean = jnp.sum(prob * s_tan, axis=-1, keepdims=True)
        prob_tan = prob * (s_tan - tan_mean)
        delta = jnp.sum(prob * d_prob, axis=-1, keepdims=True)
        delta_tan = jnp.sum(prob_tan * d_prob + prob * d_prob_tan, axis=-1, keepdims=True)
        d_score = prob * (d_prob - delta)
        d_score_tan = prob_tan * (d_prob - delta) + prob * (d_prob_tan - delta_tan)
        prob_tan_b = rounded(prob_tan)
        d_score_b = rounded(d_score)
        d_score_tan_b = rounded(d_score_tan)
        dq_part = (jnp.einsum("hgts,shd->thgd", d_score_tan_b, key_full) + jnp.einsum("hgts,shd->thgd", d_score_b, key_tan)) * scaling
        dk_part = (jnp.einsum("hgts,thgd->shd", d_score_tan_b, query_rows) + jnp.einsum("hgts,thgd->shd", d_score_b, query_tan)) * scaling
        dv_part = jnp.einsum("hgts,thgd->shd", prob_tan_b, grad_rows)
        return (dk_acc + dk_part, dv_acc + dv_part), dq_part

    empty = jnp.zeros((SEQ_LEN, KVH, HD), jnp.float32)
    (dk_total, dv_total), dq_blocks = lax.scan(one_block, (empty, empty), inputs)
    dq_tangent = dq_blocks.reshape(SEQ_LEN, QH * HD).astype(jnp.bfloat16)
    dk_tangent = dk_total.reshape(SEQ_LEN, KVH * HD).astype(jnp.bfloat16)
    dv_tangent = dv_total.reshape(SEQ_LEN, KVH * HD).astype(jnp.bfloat16)
    dq_wide = dq_tangent.astype(jnp.float32)
    dk_wide = dk_tangent.astype(jnp.float32)
    dv_wide = dv_tangent.astype(jnp.float32)
    squared_norm = jnp.sum(dq_wide * dq_wide) + jnp.sum(dk_wide * dk_wide) + jnp.sum(dv_wide * dv_wide)
    return dq_tangent, dk_tangent, dv_tangent, squared_norm
```

```python
import jax
import jax.numpy as jnp
from jax import lax
from jax.experimental import pallas as pl
from jax.experimental.pallas import tpu as pltpu
from jax.sharding import Mesh
from jax.sharding import PartitionSpec as P

HD = 128
G = 8
TOK = 128
ROWS = G * TOK
STEPS = 16
TILE = 256
CHUNK = 16
AXES = ("head", "seq_0", "seq_1", "seq_2")
SEQ = ("seq_0", "seq_1", "seq_2")
SCALE = HD ** -0.5
EXP_SCALE = SCALE * 1.4426950408889634
NEG = -1e30
F32 = jnp.float32
BF16 = jnp.bfloat16
MESH_ID = pl.DeviceIdType.MESH


def mm(a, b):
    return jnp.dot(a, b, preferred_element_type=F32)


def mm_nt(a, b):
    return lax.dot_general(a, b, (((1,), (1,)), ((), ())), preferred_element_type=F32)


def ring(i):
    return i + i // 2 - 2 * (i // 3)


def offsets(p):
    later = (p + 8) // 12
    q = (p - 4) * later
    first = p * (1 - later) + (q // 3) * later
    second = (1 + q % 3) * later
    return ring(first), ring(second)


def kernel(
    order, q_in, k_in, v_in, qt_in, kt_in, vt_in, do_in,
    dq_out, dk_out, dv_out, norm_out,
    kv, w_s, w_st, w_dp, w_dpt, w_qt,
    e_all, st_all, dp_all, dpt_all, max_all,
    run_max, run_sum, run_st, run_dp, run_cross, dq_acc,
    dst_b, ds_b, pt_b,
    pair_send, pair_recv, held, far_recv, near_recv, norm_plane, norm_line,
    g_near_s, g_far_s, g_pair_s, g_own_r, g_other_r,
    r_pair_s, r_pair_r, r_far_s, r_far_r, r_near_s, r_near_r,
    n_plane_s, n_plane_r, n_line_s, n_line_r,
):
    head, y0, x0, c0 = [lax.axis_index(n) for n in AXES]
    mine = order[(y0 * 4 + x0) * 2 + c0]

    def at(plane, a, b):
        x = lax.rem(x0 + a * (1 - plane) + b * plane, 4)
        y = lax.rem(y0 + a * plane + b * (1 - plane), 4)
        return y, x

    def device(a, b):
        y, x = at(c0, a, b)
        return (head, y, x, c0)

    partner = (head, y0, x0, 1 - c0)

    def hidden(plane, p):
        a, b = offsets(p)
        y, x = at(plane, a, b)
        return jnp.where(order[(y * 4 + x) * 2 + plane] < mine, 0.0, NEG)

    def remote(src, dst, s, r, to):
        return pltpu.make_async_remote_copy(
            src_ref=src, dst_ref=dst, send_sem=s, recv_sem=r, device_id=to, device_id_type=MESH_ID
        )

    def in_plane(dy, dx):
        y, x = lax.rem(y0 + dy, 4), lax.rem(x0 + dx, 4)
        return (head, y, x, c0), y * 4 + x

    def in_line(dz, dc):
        z, c = lax.rem(head + dz, 8), lax.rem(c0 + dc, 2)
        return (z, y0, x0, c), z * 2 + c

    far_first = lambda n, m: sorted(
        [(i, j) for i in range(n) for j in range(m) if i or j],
        key=lambda o: -(min(o[0], n - o[0]) + min(o[1], m - o[1])),
    )
    plane_peers, line_peers = far_first(4, 4), far_first(8, 2)

    barrier = pltpu.get_barrier_semaphore()
    for o in plane_peers:
        pl.semaphore_signal(barrier, inc=1, device_id=in_plane(*o)[0], device_id_type=MESH_ID)
    for o in line_peers:
        pl.semaphore_signal(barrier, inc=1, device_id=in_line(*o)[0], device_id_type=MESH_ID)

    kv[0, 0, 0] = k_in[...]
    kv[0, 1, 0] = kt_in[...]
    kv[0, 2, 0] = v_in[...]
    kv[0, 3, 0] = vt_in[...]

    pl.semaphore_wait(barrier, 30)

    back = (0, 2, 1, 3)

    def near_copy(i):
        a = (0, 1, 3, 2)[i]
        slot = back[i]
        return remote(kv.at[0, :, 0], kv.at[slot, :, 0], g_near_s.at[i], g_own_r.at[slot], device(a, 0))

    def far_copy(i, j):
        b = (0, 1, 3, 2)[j]
        slot = 4 + 3 * i + back[j] - 1
        return remote(
            kv.at[i, :, 0], kv.at[slot, :, 0], g_far_s.at[3 * i + j - 1], g_own_r.at[slot], device(0, b)
        )

    def pair_copy(p):
        return remote(kv.at[p, :, 0], kv.at[p, :, 1], g_pair_s.at[p], g_other_r.at[p], partner)

    for i in (1, 2, 3):
        near_copy(i).start()
    pair_copy(0).start()
    for j in (1, 2, 3):
        far_copy(0, j).start()

    for g in range(G):
        c = slice(g * HD, (g + 1) * HD)
        q = q_in[:, c].astype(F32)
        qs = q.T * EXP_SCALE
        hi = qs.astype(BF16)
        w_s[0:HD, c] = hi
        w_s[HD:, c] = (qs - hi.astype(F32)).astype(BF16)
        qt = qt_in[:, c]
        qt = qt.astype(F32).T
        w_st[0:HD, c] = qt.astype(BF16)
        w_qt[:, c] = (qt * (1.0 / SCALE)).astype(BF16)
        w_st[HD:, c] = q.T.astype(BF16)
        do = do_in[:, c]
        dot = do.astype(F32).T
        w_dp[:, c] = dot.astype(BF16)
        dos = dot * (1.0 / SCALE)
        hi = dos.astype(BF16)
        w_dpt[0:HD, c] = hi
        w_dpt[HD:, c] = (dos - hi.astype(F32)).astype(BF16)

    run_max[...] = jnp.full(run_max.shape, NEG, F32)
    for r in (run_sum, run_st, run_dp, run_cross):
        r[...] = jnp.zeros(r.shape, F32)
    dq_acc[...] = jnp.zeros(dq_acc.shape, F32)

    def scores(p, halves, biases, diagonal):
        n = len(halves) * TOK
        k, kt, v, vt = [kv[p, i, pl.ds(halves[0], len(halves))].reshape(n, HD) for i in range(4)]
        kk = jnp.concatenate([k, k], axis=1)
        kkt = jnp.concatenate([k, kt], axis=1)
        vvt = jnp.concatenate([vt, vt], axis=1)
        for t in range(ROWS // TILE):
            c = slice(t * TILE, (t + 1) * TILE)
            s_all = mm(kk, w_s[:, c])
            st_t = mm(kkt, w_st[:, c])
            dp_t = mm(v, w_dp[:, c])
            dpt_t = mm(vvt, w_dpt[:, c])
            new_max = run_max[t]
            parts = []
            for n_at, half in enumerate(halves):
                rows = slice(n_at * TOK, (n_at + 1) * TOK)
                s = s_all[rows]
                if diagonal:
                    key = lax.broadcasted_iota(jnp.int32, (TOK, TILE), 0)
                    tok = lax.rem(lax.broadcasted_iota(jnp.int32, (TOK, TILE), 1), TOK)
                    s = jnp.where(key <= tok, s, NEG)
                s = s.reshape(TOK // 8, 8, TILE)
                top = jnp.max(s, axis=0)
                e = jnp.exp2(s - top[None])
                e_all[p, half, t] = e.reshape(TOK, TILE).astype(BF16)
                st_all[p, half, t] = st_t[rows]
                dp_all[p, half, t] = dp_t[rows]
                dpt_b = dpt_t[rows].astype(BF16)
                dpt_all[p, half, t] = dpt_b
                st = st_t[rows].reshape(TOK // 8, 8, TILE)
                dp = dp_t[rows].reshape(TOK // 8, 8, TILE)
                dpt = dpt_b.astype(F32).reshape(TOK // 8, 8, TILE)
                es = e * st
                top = top if biases[n_at] is None else top + biases[n_at]
                max_all[p, half, t] = top
                new_max = jnp.maximum(new_max, top)
                parts.append((
                    top,
                    jnp.sum(e, axis=0),
                    jnp.sum(es, axis=0),
                    jnp.sum(e * dp, axis=0),
                    jnp.sum(es * dp, axis=0) + jnp.sum(e * dpt, axis=0),
                ))
            decay = jnp.exp2(run_max[t] - new_max)
            run_max[t] = new_max
            weights = [jnp.exp2(part[0] - new_max) for part in parts]
            for i, r in enumerate((run_sum, run_st, run_dp, run_cross)):
                total = r[t] * decay
                for part, weight in zip(parts, weights):
                    total = total + part[i + 1] * weight
                r[t] = total

    scores(0, (0,), (None,), True)
    for i in (1, 2, 3):
        near_copy(back[i]).wait_recv()
        for j in (1, 2, 3):
            far_copy(i, j).start()
        pair_copy(i).start()
    pair_copy(0).wait_recv()
    scores(0, (1,), (hidden(1 - c0, 0),), False)

    def wait_own(p):
        remote(kv.at[0, :, 0], kv.at[p, :, 0], g_pair_s.at[0], g_own_r.at[p], partner).wait_recv()

    def score_step(p, carry):
        @pl.when((p >= 3) & (p < STEPS - 1))
        def _():
            wait_own(p + 1)
            pair_copy(p + 1).start()

        pair_copy(p).wait_recv()
        scores(p, (0, 1), (hidden(c0, p), hidden(1 - c0, p)), False)
        return carry

    lax.fori_loop(1, STEPS, score_step, 0)

    top = jnp.max(run_max[...], axis=1, keepdims=True)
    weight = jnp.exp2(run_max[...] - top)
    sums = [jnp.sum(r[...] * weight, axis=1, keepdims=True) for r in (run_sum, run_st, run_dp, run_cross)]
    inverse = 1.0 / sums[0]
    st_mean = sums[1] * inverse
    delta = sums[2] * inverse
    delta_tan = sums[3] * inverse - st_mean * delta
    for r, value in ((run_max, top), (run_sum, inverse), (run_st, st_mean), (run_dp, delta), (run_cross, delta_tan)):
        r[...] = jnp.broadcast_to(value, r.shape)

    def pair_back(p):
        slot = lax.rem(p, 2)
        return remote(pair_send.at[slot], pair_recv.at[p], r_pair_s.at[slot], r_pair_r.at[p], partner)

    def far_back(p):
        a, b = offsets(p)
        return remote(pair_recv.at[p], far_recv.at[p - 4], r_far_s.at[p - 4], r_far_r.at[p - 4], device(0, b))

    def near_back(p):
        a, b = offsets(p)
        return remote(pair_recv.at[p], near_recv.at[p - 1], r_near_s.at[p - 1], r_near_r.at[p - 1], device(a, 0))

    def summed(p):
        pair_back(p).wait_recv()
        return held[lax.rem(p, 2)] + pair_recv[p].astype(F32)

    def with_far(p, total):
        for j in range(3):
            far_back(4 + 3 * p + j).wait_recv()
            total = total + far_recv[3 * p + j].astype(F32)
        return total

    def send_on(p):
        @pl.when(p >= 4)
        def _():
            pair_recv[p] = summed(p).astype(BF16)
            far_back(p).start()

        @pl.when(p < 4)
        def _():
            pair_recv[p] = with_far(p, summed(p)).astype(BF16)
            near_back(p).start()

    def terms(p):
        def two_tiles(i, carry):
            for t in (2 * i, 2 * i + 1):
                for half in (0, 1):
                    f = jnp.exp2(max_all[p, half, t] - run_max[t]) * run_sum[t]
                    st_mean, delta, delta_tan = run_st[t], run_dp[t], run_cross[t]
                    for at_row in range(0, TOK, CHUNK):
                        from_rows = slice(at_row, at_row + CHUNK)
                        to_rows = slice(half * TOK + at_row, half * TOK + at_row + CHUNK)
                        shape = (CHUNK // 8, 8, TILE)
                        prob = e_all[p, half, t, from_rows].astype(F32).reshape(shape) * f[None]
                        u = st_all[p, half, t, from_rows].reshape(shape) - st_mean[None]
                        v = dp_all[p, half, t, from_rows].reshape(shape) - delta[None]
                        w = dpt_all[p, half, t, from_rows].astype(F32).reshape(shape) - delta_tan[None]
                        pt = prob * u
                        for place, value in ((dst_b, pt * v + prob * w), (ds_b, prob * v), (pt_b, pt)):
                            place[t, to_rows] = value.reshape(CHUNK, TILE).astype(BF16)
            return carry

        lax.fori_loop(0, ROWS // TILE // 2, two_tiles, 0)

    def products(p):
        k = kv[p, 0].reshape(2 * TOK, HD)
        kt = (kv[p, 1].reshape(2 * TOK, HD).astype(F32) * (1.0 / SCALE)).astype(BF16)
        keys = jnp.concatenate([k.T, kt.T], axis=1)
        dk = dv = 0.0
        for t in range(ROWS // TILE):
            c = slice(t * TILE, (t + 1) * TILE)
            dq_acc[t] += mm(keys, jnp.concatenate([dst_b[t], ds_b[t]], axis=0))
            q_both = jnp.concatenate([w_st[HD:, c], w_qt[:, c]], axis=1)
            dk = dk + mm_nt(q_both, jnp.concatenate([dst_b[t], ds_b[t]], axis=1))
            dv = dv + mm_nt(w_dp[:, c], pt_b[t])
        return jnp.concatenate([dk * (SCALE * SCALE), dv * SCALE], axis=0)

    def hand_over(p, both):
        @pl.when(p < STEPS - 2)
        def _():
            pair_back(p).wait_send()

        held[lax.rem(p, 2)] = both[:, :TOK]
        pair_send[lax.rem(p, 2)] = both[:, TOK:].astype(BF16)
        pair_back(p).start()

        @pl.when(p < STEPS - 1)
        def _():
            send_on(p + 1)

    def grad_step(i, carry):
        p = STEPS - 1 - i
        terms(p)
        hand_over(p, products(p))
        return carry

    lax.fori_loop(0, STEPS, grad_step, 0)

    norm = jnp.zeros((8, HD), F32)
    for g in range(G):
        c = slice(g * HD, (g + 1) * HD)
        dq = (dq_acc[g // 2, :, (g % 2) * HD : (g % 2 + 1) * HD] * (SCALE * SCALE)).T.astype(BF16)
        dq_out[:, c] = dq
        wide = dq.astype(F32)
        norm = norm + jnp.sum((wide * wide).reshape(TOK // 8, 8, HD), axis=0)
    total = with_far(0, summed(0))
    for p in (1, 2, 3):
        near_back(p).wait_recv()
        total = total + near_recv[p - 1].astype(F32)
    for out, value in ((dk_out, total[:HD]), (dv_out, total[HD:])):
        value = value.T.astype(BF16)
        out[...] = value
        wide = value.astype(F32)
        norm = norm + jnp.sum((wide * wide).reshape(TOK // 8, 8, HD), axis=0)
    for buffer, place, peers, me, sent, got in (
        (norm_plane, in_plane, plane_peers, y0 * 4 + x0, n_plane_s, n_plane_r),
        (norm_line, in_line, line_peers, head * 2 + c0, n_line_s, n_line_r),
    ):
        buffer[me] = norm
        copies = [
            remote(buffer.at[me], buffer.at[me], sent.at[i], got.at[me], place(*o)[0]) for i, o in enumerate(peers)
        ]
        for copy in copies:
            copy.start()
        for i, o in enumerate(peers):
            to, other = place(*o)
            remote(buffer.at[me], buffer.at[other], sent.at[i], got.at[other], to).wait_recv()
        norm = buffer[0]
        for i in range(1, 16):
            norm = norm + buffer[i]
        for copy in copies:
            copy.wait_send()
    norm_out[0, 0] = jnp.sum(norm)

    for i in (1, 2, 3):
        near_copy(i).wait_send()
    for i in range(4):
        for j in (1, 2, 3):
            far_copy(i, j).wait_send()
    for p in range(STEPS):
        pair_copy(p).wait_send()
    for p in (0, 1):
        pair_back(p).wait_send()
    for p in range(4, STEPS):
        far_back(p).wait_send()
    for p in (1, 2, 3):
        near_back(p).wait_send()


def body(queries, keys, values, q_tangent, k_tangent, v_tangent, out_grad, block_order):
    vmem = pl.BlockSpec(memory_space=pltpu.VMEM)
    stored = lambda dtype: pltpu.VMEM((STEPS, 2, ROWS // TILE, TOK, TILE), dtype)
    row = pltpu.VMEM((ROWS // TILE, 8, TILE), F32)
    sem = lambda n: pltpu.SemaphoreType.DMA((n,))
    dq, dk, dv, norm = pl.pallas_call(
        kernel,
        out_shape=(
            jax.ShapeDtypeStruct((TOK, ROWS), BF16),
            jax.ShapeDtypeStruct((TOK, HD), BF16),
            jax.ShapeDtypeStruct((TOK, HD), BF16),
            jax.ShapeDtypeStruct((1, 1), F32),
        ),
        in_specs=[pl.BlockSpec(memory_space=pltpu.SMEM)] + [vmem] * 7,
        out_specs=(vmem,) * 3 + (pl.BlockSpec(memory_space=pltpu.SMEM),),
        scratch_shapes=[
            pltpu.VMEM((STEPS, 4, 2, TOK, HD), BF16),
            pltpu.VMEM((2 * HD, ROWS), BF16),
            pltpu.VMEM((2 * HD, ROWS), BF16),
            pltpu.VMEM((HD, ROWS), BF16),
            pltpu.VMEM((2 * HD, ROWS), BF16),
            pltpu.VMEM((HD, ROWS), BF16),
            stored(BF16),
            stored(F32),
            stored(F32),
            stored(BF16),
            pltpu.VMEM((STEPS, 2, ROWS // TILE, 8, TILE), F32),
            row, row, row, row, row,
            pltpu.VMEM((ROWS // TILE, HD, TILE), F32),
            pltpu.VMEM((ROWS // TILE, 2 * TOK, TILE), BF16),
            pltpu.VMEM((ROWS // TILE, 2 * TOK, TILE), BF16),
            pltpu.VMEM((ROWS // TILE, 2 * TOK, TILE), BF16),
            pltpu.VMEM((2, 2 * HD, TOK), BF16),
            pltpu.VMEM((STEPS, 2 * HD, TOK), BF16),
            pltpu.VMEM((2, 2 * HD, TOK), F32),
            pltpu.VMEM((12, 2 * HD, TOK), BF16),
            pltpu.VMEM((3, 2 * HD, TOK), BF16),
            pltpu.VMEM((16, 8, HD), F32),
            pltpu.VMEM((16, 8, HD), F32),
            sem(4), sem(12), sem(STEPS), sem(STEPS), sem(STEPS),
            sem(2), sem(STEPS), sem(12), sem(12), sem(3), sem(3),
            sem(15), sem(16), sem(15), sem(16),
        ],
        compiler_params=pltpu.CompilerParams(
            collective_id=0, has_side_effects=True, vmem_limit_bytes=63 * 2**20
        ),
    )(block_order, queries, keys, values, q_tangent, k_tangent, v_tangent, out_grad)
    return dq, dk, dv, norm.reshape(())


def solution(mesh):
    torus = Mesh(mesh.devices.reshape(mesh.shape["head"], 4, 4, 2), AXES)
    split = P(SEQ, "head")
    return jax.shard_map(
        body,
        mesh=torus,
        in_specs=(split,) * 7 + (P(),),
        out_specs=(split,) * 3 + (P(),),
        check_vma=False,
    )
```

```python
import jax
import jax.numpy as jnp
from jax import lax
from jax.experimental import pallas as pl
from jax.experimental.pallas import tpu as pltpu
from jax.sharding import Mesh
from jax.sharding import PartitionSpec as P

HD = 128
G = 8
TOK = 128
ROWS = G * TOK
STEPS = 16
TILE = 256
AXES = ("head", "seq_0", "seq_1", "seq_2")
SEQ = ("seq_0", "seq_1", "seq_2")
SCALE = HD ** -0.5
EXP_SCALE = SCALE * 1.4426950408889634
NEG = -1e30
F32 = jnp.float32
BF16 = jnp.bfloat16
MESH_ID = pl.DeviceIdType.MESH


def mm(a, b):
    return jnp.dot(a, b, preferred_element_type=F32)


def ring(i):
    return i + i // 2 - 2 * (i // 3)


def offsets(p):
    later = (p + 8) // 12
    q = (p - 4) * later
    first = p * (1 - later) + (q // 3) * later
    second = (1 + q % 3) * later
    return ring(first), ring(second)


def kernel(
    order, q_hbm, k_in, v_in, qt_hbm, kt_in, vt_in, do_hbm,
    dq_hbm, dk_hbm, dv_hbm, norm_out,
    q_in, qt_in, do_in, dq_out, dk_out, dv_out, in_sem, out_sem,
    kv, w_st, w_dp, q_rows, do_rows,
    e_all, st_all, dp_all, dpt_all, max_all,
    run_max, run_sum, run_st, run_dp, run_cross, dq_acc,
    pair_send, pair_recv, held, far_recv, near_recv, norm_plane, norm_line,
    g_near_s, g_far_s, g_pair_s, g_own_r, g_other_r,
    r_pair_s, r_pair_r, r_far_s, r_far_r, r_near_s, r_near_r,
    n_plane_s, n_plane_r, n_line_s, n_line_r,
):
    head, y0, x0, c0 = [lax.axis_index(n) for n in AXES]
    mine = order[(y0 * 4 + x0) * 2 + c0]

    def at(plane, a, b):
        x = lax.rem(x0 + a * (1 - plane) + b * plane, 4)
        y = lax.rem(y0 + a * plane + b * (1 - plane), 4)
        return y, x

    def device(a, b):
        y, x = at(c0, a, b)
        return (head, y, x, c0)

    partner = (head, y0, x0, 1 - c0)

    def hidden(plane, p):
        a, b = offsets(p)
        y, x = at(plane, a, b)
        return jnp.where(order[(y * 4 + x) * 2 + plane] < mine, 0.0, NEG)

    def remote(src, dst, s, r, to):
        return pltpu.make_async_remote_copy(
            src_ref=src, dst_ref=dst, send_sem=s, recv_sem=r, device_id=to, device_id_type=MESH_ID
        )

    arrivals = [
        pltpu.make_async_copy(src, dst, in_sem.at[i])
        for i, (src, dst) in enumerate((
            (k_in, kv.at[0, 0, 0]), (kt_in, kv.at[0, 1, 0]), (v_in, kv.at[0, 2, 0]), (vt_in, kv.at[0, 3, 0]),
            (q_hbm, q_in), (qt_hbm, qt_in), (do_hbm, do_in),
        ))
    ]
    for arrival in arrivals:
        arrival.start()

    def in_plane(dy, dx):
        y, x = lax.rem(y0 + dy, 4), lax.rem(x0 + dx, 4)
        return (head, y, x, c0), y * 4 + x

    def in_line(dz, dc):
        z, c = lax.rem(head + dz, 8), lax.rem(c0 + dc, 2)
        return (z, y0, x0, c), z * 2 + c

    far_first = lambda n, m: sorted(
        [(i, j) for i in range(n) for j in range(m) if i or j],
        key=lambda o: -(min(o[0], n - o[0]) + min(o[1], m - o[1])),
    )
    plane_peers, line_peers = far_first(4, 4), far_first(8, 2)

    barrier = pltpu.get_barrier_semaphore()
    for o in plane_peers:
        pl.semaphore_signal(barrier, inc=1, device_id=in_plane(*o)[0], device_id_type=MESH_ID)
    for o in line_peers:
        pl.semaphore_signal(barrier, inc=1, device_id=in_line(*o)[0], device_id_type=MESH_ID)

    for arrival in arrivals:
        arrival.wait()

    for g in range(G):
        c = slice(g * HD, (g + 1) * HD)
        q = q_in[:, c].astype(F32)
        qt = qt_in[:, c]
        w_st[0:HD, c] = qt.astype(F32).T.astype(BF16)
        w_st[HD:, c] = q.T.astype(BF16)
        do = do_in[:, c]
        w_dp[:, c] = do.astype(F32).T.astype(BF16)
        q_rows[g // 2, pl.ds((g % 2) * TOK, TOK), :] = q_in[:, c]
        q_rows[g // 2, pl.ds(2 * TOK + (g % 2) * TOK, TOK), :] = (qt.astype(F32) * (1.0 / SCALE)).astype(BF16)
        do_rows[c, :] = do

    run_max[...] = jnp.full(run_max.shape, NEG, F32)
    for r in (run_sum, run_st, run_dp, run_cross):
        r[...] = jnp.zeros(r.shape, F32)
    dq_acc[...] = jnp.zeros(dq_acc.shape, F32)
    pl.semaphore_wait(barrier, 30)

    back = (0, 2, 1, 3)

    def near_copy(i):
        a = (0, 1, 3, 2)[i]
        slot = back[i]
        return remote(kv.at[0, :, 0], kv.at[slot, :, 0], g_near_s.at[i], g_own_r.at[slot], device(a, 0))

    def far_copy(i, j):
        b = (0, 1, 3, 2)[j]
        slot = 4 + 3 * i + back[j] - 1
        return remote(
            kv.at[i, :, 0], kv.at[slot, :, 0], g_far_s.at[3 * i + j - 1], g_own_r.at[slot], device(0, b)
        )

    def pair_copy(p):
        return remote(kv.at[p, :, 0], kv.at[p, :, 1], g_pair_s.at[p], g_other_r.at[p], partner)

    for i in (1, 2, 3):
        near_copy(i).start()
    pair_copy(0).start()

    def scores(p, halves, biases, diagonal):
        n = len(halves) * TOK
        k, kt, v, vt = [kv[p, i, pl.ds(halves[0], len(halves))].reshape(n, HD) for i in range(4)]
        kkt = jnp.concatenate([k, kt], axis=1)
        vvt = jnp.concatenate([v, vt], axis=0)
        for t in range(ROWS // TILE):
            c = slice(t * TILE, (t + 1) * TILE)
            s_all = mm(k, w_st[HD:, c])
            st_t = mm(kkt, w_st[:, c])
            both = mm(vvt, w_dp[:, c])
            dp_t, dpt_t = both[:n], both[n:] * (1.0 / SCALE)
            new_max = run_max[t]
            parts = []
            for n_at, half in enumerate(halves):
                rows = slice(n_at * TOK, (n_at + 1) * TOK)
                s = s_all[rows]
                if diagonal:
                    key = lax.broadcasted_iota(jnp.int32, (TOK, TILE), 0)
                    tok = lax.rem(lax.broadcasted_iota(jnp.int32, (TOK, TILE), 1), TOK)
                    s = jnp.where(key <= tok, s, NEG)
                s = s.reshape(TOK // 8, 8, TILE)
                top = jnp.max(s, axis=0)
                e = jnp.exp2((s - top[None]) * EXP_SCALE)
                top = top * EXP_SCALE
                e_all[p, half, t] = e.reshape(TOK, TILE).astype(BF16)
                st_all[p, half, t] = st_t[rows]
                dp_all[p, half, t] = dp_t[rows]
                dpt_b = dpt_t[rows].astype(BF16)
                dpt_all[p, half, t] = dpt_b
                st = st_t[rows].reshape(TOK // 8, 8, TILE)
                dp = dp_t[rows].reshape(TOK // 8, 8, TILE)
                dpt = dpt_b.astype(F32).reshape(TOK // 8, 8, TILE)
                es = e * st
                top = top if biases[n_at] is None else top + biases[n_at]
                max_all[p, half, t] = top
                new_max = jnp.maximum(new_max, top)
                parts.append((
                    top,
                    jnp.sum(e, axis=0),
                    jnp.sum(es, axis=0),
                    jnp.sum(e * dp, axis=0),
                    jnp.sum(es * dp, axis=0) + jnp.sum(e * dpt, axis=0),
                ))
            decay = jnp.exp2(run_max[t] - new_max)
            run_max[t] = new_max
            weights = [jnp.exp2(part[0] - new_max) for part in parts]
            for i, r in enumerate((run_sum, run_st, run_dp, run_cross)):
                total = r[t] * decay
                for part, weight in zip(parts, weights):
                    total = total + part[i + 1] * weight
                r[t] = total

    scores(0, (0,), (None,), True)
    for i in (1, 2, 3):
        near_copy(i).wait_send()
    for j in (1, 2, 3):
        far_copy(0, j).start()
    for i in (1, 2, 3):
        near_copy(back[i]).wait_recv()
        for j in (1, 2, 3):
            far_copy(i, j).start()
        pair_copy(i).start()
    pair_copy(0).wait_recv()
    scores(0, (1,), (hidden(1 - c0, 0),), False)

    def wait_own(p):
        remote(kv.at[0, :, 0], kv.at[p, :, 0], g_pair_s.at[0], g_own_r.at[p], partner).wait_recv()

    def score_step(p, carry):
        @pl.when((p >= 3) & (p < STEPS - 1))
        def _():
            wait_own(p + 1)
            pair_copy(p + 1).start()

        pair_copy(p).wait_recv()
        scores(p, (0, 1), (hidden(c0, p), hidden(1 - c0, p)), False)
        return carry

    lax.fori_loop(1, STEPS, score_step, 0)

    top = jnp.max(run_max[...], axis=1, keepdims=True)
    weight = jnp.exp2(run_max[...] - top)
    sums = [jnp.sum(r[...] * weight, axis=1, keepdims=True) for r in (run_sum, run_st, run_dp, run_cross)]
    inverse = 1.0 / sums[0]
    st_mean = sums[1] * inverse
    delta = sums[2] * inverse
    delta_tan = sums[3] * inverse - st_mean * delta
    for r, value in ((run_max, top), (run_sum, inverse), (run_st, st_mean), (run_dp, delta), (run_cross, delta_tan)):
        r[...] = jnp.broadcast_to(value, r.shape)

    def pair_back(p):
        slot = lax.rem(p, 2)
        return remote(pair_send.at[slot], pair_recv.at[p], r_pair_s.at[slot], r_pair_r.at[p], partner)

    def far_back(p):
        a, b = offsets(p)
        return remote(pair_recv.at[p], far_recv.at[p - 4], r_far_s.at[p - 4], r_far_r.at[p - 4], device(0, b))

    def near_back(p):
        a, b = offsets(p)
        return remote(pair_recv.at[p], near_recv.at[p - 1], r_near_s.at[p - 1], r_near_r.at[p - 1], device(a, 0))

    def summed(p):
        pair_back(p).wait_recv()
        return held[lax.rem(p, 2)] + pair_recv[p].astype(F32)

    def with_far(p, total):
        for j in range(3):
            far_back(4 + 3 * p + j).wait_recv()
            total = total + far_recv[3 * p + j].astype(F32)
        return total

    def send_on(p):
        @pl.when(p >= 4)
        def _():
            pair_recv[p] = summed(p).astype(BF16)
            far_back(p).start()

        @pl.when(p < 4)
        def _():
            pair_recv[p] = with_far(p, summed(p)).astype(BF16)
            near_back(p).start()

    def grad_step(i, carry):
        p = STEPS - 1 - i
        dk = jnp.zeros((2 * TOK, HD), F32)
        dv = jnp.zeros((2 * TOK, HD), F32)
        for t in range(ROWS // TILE):
            c = slice(t * TILE, (t + 1) * TILE)
            made = []
            for half in (0, 1):
                f = jnp.exp2(max_all[p, half, t] - run_max[t]) * run_sum[t]
                shape = (TOK // 8, 8, TILE)
                prob = e_all[p, half, t].astype(F32).reshape(shape) * f[None]
                u = st_all[p, half, t].reshape(shape) - run_st[t][None]
                v = dp_all[p, half, t].reshape(shape) - run_dp[t][None]
                w = dpt_all[p, half, t].astype(F32).reshape(shape) - run_cross[t][None]
                pt = prob * u
                made.append([
                    x.reshape(TOK, TILE).astype(BF16) for x in (pt * v + prob * w, prob * v, pt)
                ])
            dst, ds, pt = [jnp.concatenate(x, axis=0) for x in zip(*made)]
            for half in (0, 1):
                rows = slice(half * TOK, (half + 1) * TOK)
                dpt_all[p, half, t] = dst[rows]
                e_all[p, half, t] = ds[rows]
            dk = dk + mm(jnp.concatenate([dst, ds], axis=1), q_rows[t])
            dv = dv + mm(pt, do_rows[c, :])
        both = jnp.concatenate([dk * (SCALE * SCALE), dv * SCALE], axis=1)

        @pl.when(i >= 2)
        def _():
            pair_back(p).wait_send()

        held[lax.rem(p, 2)] = both[:TOK]
        pair_send[lax.rem(p, 2)] = both[TOK:].astype(BF16)
        pair_back(p).start()

        @pl.when(i >= 1)
        def _():
            send_on(p + 1)

        return carry

    lax.fori_loop(0, STEPS, grad_step, 0)

    def query_step(i, carry):
        sides = []
        for p in (2 * i, 2 * i + 1):
            k = kv[p, 0].reshape(2 * TOK, HD)
            kt = (kv[p, 1].reshape(2 * TOK, HD).astype(F32) * (1.0 / SCALE)).astype(BF16)
            sides += [k.T, kt.T]
        keys = jnp.concatenate(sides, axis=1)
        for t in range(ROWS // TILE):
            terms = []
            for p in (2 * i, 2 * i + 1):
                terms += [dpt_all[p, :, t].reshape(2 * TOK, TILE), e_all[p, :, t].reshape(2 * TOK, TILE)]
            dq_acc[t] += mm(keys, jnp.concatenate(terms, axis=0))
        return carry

    lax.fori_loop(0, STEPS // 2, query_step, 0)

    norm = jnp.zeros((8, HD), F32)
    for g in range(G):
        c = slice(g * HD, (g + 1) * HD)
        dq = (dq_acc[g // 2, :, (g % 2) * HD : (g % 2 + 1) * HD] * (SCALE * SCALE)).T.astype(BF16)
        dq_out[:, c] = dq
        wide = dq.astype(F32)
        norm = norm + jnp.sum((wide * wide).reshape(TOK // 8, 8, HD), axis=0)
    departures = [
        pltpu.make_async_copy(src, dst, out_sem.at[i])
        for i, (src, dst) in enumerate(((dq_out, dq_hbm), (dk_out, dk_hbm), (dv_out, dv_hbm)))
    ]
    departures[0].start()
    total = with_far(0, summed(0))
    for p in (1, 2, 3):
        near_back(p).wait_recv()
        total = total + near_recv[p - 1].astype(F32)
    for out, value in ((dk_out, total[:, :HD]), (dv_out, total[:, HD:])):
        value = value.astype(BF16)
        out[...] = value
        wide = value.astype(F32)
        norm = norm + jnp.sum((wide * wide).reshape(TOK // 8, 8, HD), axis=0)
    departures[1].start()
    departures[2].start()
    sends = []
    for buffer, place, peers, me, sent, got in (
        (norm_plane, in_plane, plane_peers, y0 * 4 + x0, n_plane_s, n_plane_r),
        (norm_line, in_line, line_peers, head * 2 + c0, n_line_s, n_line_r),
    ):
        buffer[me] = norm
        copies = [
            remote(buffer.at[me], buffer.at[me], sent.at[i], got.at[me], place(*o)[0]) for i, o in enumerate(peers)
        ]
        for copy in copies:
            copy.start()
        for i, o in enumerate(peers):
            to, other = place(*o)
            remote(buffer.at[me], buffer.at[other], sent.at[i], got.at[other], to).wait_recv()
        norm = buffer[0]
        for i in range(1, 16):
            norm = norm + buffer[i]
        sends += copies
    norm_out[0, 0] = jnp.sum(norm)
    for copy in sends:
        copy.wait_send()
    for departure in departures:
        departure.wait()

    for i in range(4):
        for j in (1, 2, 3):
            far_copy(i, j).wait_send()
    for p in range(STEPS):
        pair_copy(p).wait_send()
    for p in (0, 1):
        pair_back(p).wait_send()
    for p in range(4, STEPS):
        far_back(p).wait_send()
    for p in (1, 2, 3):
        near_back(p).wait_send()


def hand_on(*refs):
    for src, dst in zip(refs[:3], refs[3:]):
        dst[...] = src[...]


def body(queries, keys, values, q_tangent, k_tangent, v_tangent, out_grad, block_order):
    hbm = pl.BlockSpec(memory_space=pl.ANY)
    stored = lambda dtype: pltpu.VMEM((STEPS, 2, ROWS // TILE, TOK, TILE), dtype)
    row = pltpu.VMEM((ROWS // TILE, 8, TILE), F32)
    sem = lambda n: pltpu.SemaphoreType.DMA((n,))
    dq, dk, dv, norm = pl.pallas_call(
        kernel,
        out_shape=(
            jax.ShapeDtypeStruct((TOK, ROWS), BF16),
            jax.ShapeDtypeStruct((TOK, HD), BF16),
            jax.ShapeDtypeStruct((TOK, HD), BF16),
            jax.ShapeDtypeStruct((1, 1), F32),
        ),
        in_specs=[pl.BlockSpec(memory_space=pltpu.SMEM)] + [hbm] * 7,
        out_specs=(hbm,) * 3 + (pl.BlockSpec(memory_space=pltpu.SMEM),),
        scratch_shapes=[
            pltpu.VMEM((TOK, ROWS), BF16),
            pltpu.VMEM((TOK, ROWS), BF16),
            pltpu.VMEM((TOK, ROWS), BF16),
            pltpu.VMEM((TOK, ROWS), BF16),
            pltpu.VMEM((TOK, HD), BF16),
            pltpu.VMEM((TOK, HD), BF16),
            sem(7), sem(3),
            pltpu.VMEM((STEPS, 4, 2, TOK, HD), BF16),
            pltpu.VMEM((2 * HD, ROWS), BF16),
            pltpu.VMEM((HD, ROWS), BF16),
            pltpu.VMEM((G // 2, 4 * TOK, HD), BF16),
            pltpu.VMEM((ROWS, HD), BF16),
            stored(BF16),
            stored(F32),
            stored(F32),
            stored(BF16),
            pltpu.VMEM((STEPS, 2, ROWS // TILE, 8, TILE), F32),
            row, row, row, row, row,
            pltpu.VMEM((ROWS // TILE, HD, TILE), F32),
            pltpu.VMEM((2, TOK, 2 * HD), BF16),
            pltpu.VMEM((STEPS, TOK, 2 * HD), BF16),
            pltpu.VMEM((2, TOK, 2 * HD), F32),
            pltpu.VMEM((12, TOK, 2 * HD), BF16),
            pltpu.VMEM((3, TOK, 2 * HD), BF16),
            pltpu.VMEM((16, 8, HD), F32),
            pltpu.VMEM((16, 8, HD), F32),
            sem(4), sem(12), sem(STEPS), sem(STEPS), sem(STEPS),
            sem(2), sem(STEPS), sem(12), sem(12), sem(3), sem(3),
            sem(15), sem(16), sem(15), sem(16),
        ],
        compiler_params=pltpu.CompilerParams(
            collective_id=0, has_side_effects=True, vmem_limit_bytes=63 * 2**20
        ),
    )(block_order, queries, keys, values, q_tangent, k_tangent, v_tangent, out_grad)
    vmem = pl.BlockSpec(memory_space=pltpu.VMEM)
    dq, dk, dv = pl.pallas_call(
        hand_on,
        out_shape=tuple(jax.ShapeDtypeStruct(x.shape, x.dtype) for x in (dq, dk, dv)),
        in_specs=[vmem] * 3,
        out_specs=(vmem,) * 3,
    )(dq, dk, dv)
    return dq, dk, dv, norm.reshape(())


def solution(mesh):
    torus = Mesh(mesh.devices.reshape(mesh.shape["head"], 4, 4, 2), AXES)
    split = P(SEQ, "head")
    return jax.shard_map(
        body,
        mesh=torus,
        in_specs=(split,) * 7 + (P(),),
        out_specs=(split,) * 3 + (P(),),
        check_vma=False,
    )
```
